32 devices in a mesh: dp: 16 (over z, x, core), rep: 2 (over y).
Axes of the slice: x: 2, y: 2, z: 4, core: 2. Of those that a mesh axis runs over, the one named last changes fastest.
Arguments:
- grad_out: bfloat16 [12288, 2048], P('dp', 'rep'), may hold values from -6 to 6
- pre_act: bfloat16 [12288, 3072], P('dp', 'rep'), may hold values from -6 to 6
- up_weight: bfloat16 [3072, 2048], P('rep'), may hold values from -0.125 to 0.125
- down_weight: bfloat16 [2048, 3072], P(None, 'rep'), may hold values from -0.109375 to 0.109375
- slot_counts: int32 [16], P('dp'), may hold values from 384 to 768, as said below
Outputs:
- input_grad: bfloat16 [12288, 2048], P('dp')
- down_grad: float32 [2048, 3072], P('dp', 'rep')
The draws below stay inside these ranges and needn't reach their ends.
Inputs may be any that keep to these rules, and one draw needn't show every extreme that they name: Row i * 768 + j is live exactly when j < slot_counts[i]; some index has all 768 slots live and some index exactly 384.
All inputs are finite; a program needn't handle non-finite values.
Results may differ from the reference program's by a relative error of at most 0.0049.
Values may be sent and summed in bfloat16 or wider, within the bound.
A program may use at most 128 MiB of HBM per device.

```python
import jax
import jax.numpy as jnp
from jax import lax

D = 2048
FF = 3072
CAP = 768
ROWS = 12288
N_DP = 16


def draw_slot_counts(key, part):
    counts = jax.random.randint(key, (N_DP,), CAP // 2, CAP + 1)
    fullest = jax.random.randint(jax.random.fold_in(key, 1), (), 0, N_DP)
    step_away = jax.random.randint(jax.random.fold_in(key, 2), (), 1, max(N_DP, 2))
    emptiest = (fullest + step_away) % N_DP
    counts = counts.at[emptiest].set(CAP // 2)
    counts = counts.at[fullest].set(CAP)
    return counts.astype(jnp.int32)


def with_spikes(values, rng, source, target, shards_of, factor):
    def block_of(axis_at):
        return (jnp.arange(values.shape[axis_at]) // (values.shape[axis_at] // shards_of)).reshape((-1,) + (1,) * (values.ndim - 1 - axis_at))

    near = jax.random.permutation(rng, shards_of)[block_of(target)]
    other_side = (block_of(target) + shards_of // 2) % shards_of
    return jnp.where((block_of(source) == near) | (block_of(source) == other_side), factor * values, values)


def shard_levels(key, shape, cuts, smallest, high):
    def one(axis_at, parts):
        heights = jax.random.uniform(jax.random.fold_in(jax.random.fold_in(key, 6), axis_at), (parts,), jnp.float32, smallest / len(cuts), high / len(cuts))
        return jnp.repeat(jnp.exp(heights), shape[axis_at] // parts).reshape((-1,) + (1,) * (len(shape) - axis_at - 1))

    loudness = one(*cuts[0])
    for cut in cuts[1:]:
        loudness = loudness * one(*cut)
    return loudness


def normal_values(own_key, shape, deviation, most, cuts=(), kind=jnp.bfloat16):
    drawn = deviation * jax.random.normal(own_key, shape, jnp.float32)
    if cuts:
        drawn = drawn * shard_levels(own_key, shape, cuts, -0.22, 0.18)
    return jnp.clip(drawn, -most, most).astype(kind)


def noise_with(own_key, extent, width, limit, shards, heavy, dtype=jnp.bfloat16):
    entries = width * jax.random.normal(own_key, extent, jnp.float32)
    if shards:
        entries = entries * shard_levels(own_key, extent, shards, -0.22, 0.18)
    return jnp.clip(with_spikes(entries, jax.random.fold_in(own_key, 3), *heavy), -limit, limit).astype(dtype)


def setup_inputs(seed: int = 0) -> dict:
    splits = jax.random.split(jax.random.key(seed), 6)
    grad_out = noise_with(splits[0], (ROWS, D), 1.0, 6.0, ((0, 16), (1, 2)), (0, 1, 16, 2.0))
    pre_act = normal_values(splits[1], (ROWS, FF), 1.0, 6.0, ((0, 16), (1, 2)))
    up_weight = normal_values(splits[2], (FF, D), D ** -0.5, 0.125, ((0, 2),))
    down_weight = normal_values(splits[3], (D, FF), FF ** -0.5, 0.109375, ((1, 2),))
    slot_counts = draw_slot_counts(jax.random.fold_in(splits[5], 71), 0)
    return {"grad_out": grad_out, "pre_act": pre_act, "up_weight": up_weight, "down_weight": down_weight, "slot_counts": slot_counts}


def reference(grad_out, pre_act, up_weight, down_weight, slot_counts):
    row_index = lax.iota(jnp.int32, N_DP * CAP)
    live_rows = ((row_index % CAP) < slot_counts[row_index // CAP])[:, None]
    grad_live = jnp.where(live_rows, grad_out, jnp.zeros_like(grad_out))
    zero_pre = jnp.zeros_like(pre_act)
    hidden = jnp.where(live_rows, jnp.maximum(pre_act, zero_pre), zero_pre)
    down_grad = jnp.dot(grad_live.T, hidden, preferred_element_type=jnp.float32) / N_DP
    hidden_grad = jnp.dot(grad_live, down_weight, preferred_element_type=jnp.float32)
    pre_grad = jnp.where(pre_act > 0, hidden_grad, jnp.zeros_like(hidden_grad)).astype(jnp.bfloat16)
    input_grad = jnp.dot(pre_grad, up_weight, preferred_element_type=jnp.float32).astype(jnp.bfloat16)
    return input_grad, down_grad
```

```python
import functools

import jax
import jax.numpy as jnp
from jax import lax
from jax.experimental import pallas as pl
from jax.experimental.pallas import tpu as pltpu
from jax.sharding import PartitionSpec as P

MESH = pl.DeviceIdType.MESH
CHUNK = 128


def tile_of(extent):
    return next(t for t in (512, 384, 256, 128) if extent % t == 0)


def kernel(n_dp, n_rep, counts, grad, pre, up, down, ig_out, dg_out,
           gfull, hid, up_all, down_v, terms, from_core, from_x, from_z, masked, own_sum, other_sum,
           far_sem, load_sem, gp_send, gp_recv, g_send, g_recv, p_send, p_recv, uy_send, u_send, u_recv,
           c_send, c_recv, x_send, x_recv, z_send, z_recv):
    rows, d_own = grad.shape
    ff = pre.shape[1]
    d_all = down.shape[0]
    n_z = n_dp // 4
    z_own = n_z // n_rep
    blk = d_all // n_dp
    n_chunks = rows // CHUNK
    ff_tile, d_tile = tile_of(ff), tile_of(d_all)
    n_tiles = ff // ff_tile
    slice_rows = n_dp
    while ff % (slice_rows * 16):
        slice_rows //= 2
    slice_cols = n_dp // slice_rows
    tall, wide = ff // slice_rows, d_all // slice_cols

    me = lax.axis_index("dp")
    rep = lax.axis_index("rep")
    my_z, my_x, my_c = me // 4, (me // 2) % 2, me % 2
    core_peer = {"dp": my_z * 4 + my_x * 2 + (1 - my_c)}
    x_peer = {"dp": my_z * 4 + (1 - my_x) * 2 + my_c}
    rep_peers = [lax.rem(rep + o, n_rep) for o in range(1, n_rep)]
    above, below = my_z + 1 < n_z, my_z > 0

    def z_peer(z):
        return {"dp": z * 4 + my_x * 2 + my_c}

    def signal(sem, peer):
        pl.semaphore_signal(sem, inc=1, device_id=peer, device_id_type=MESH)

    barrier = pltpu.get_barrier_semaphore()
    near = [{"rep": r} for r in rep_peers] + [core_peer, x_peer]
    for peer in near:
        signal(barrier, peer)
    pl.when(above)(lambda: signal(barrier, z_peer(my_z + 1)))
    pl.when(below)(lambda: signal(barrier, z_peer(my_z - 1)))

    loads = [
        pltpu.make_async_copy(src, dst, load_sem.at[i])
        for i, (src, dst) in enumerate(
            ((grad, gfull.at[rep]), (pre, hid), (down, down_v), (up, up_all.at[rep])))
    ]
    loads[1].start()
    loads[0].start()
    pl.semaphore_wait(barrier, len(near) + above.astype(jnp.int32) + below.astype(jnp.int32))

    def rows_of(c):
        return pl.ds(pl.multiple_of(c * CHUNK, CHUNK), CHUNK)

    last_cols = pl.ds((z_own - 1) * 4 * blk, 4 * blk)

    def grad_copy(c, o, source):
        return pltpu.make_async_remote_copy(
            src_ref=grad.at[rows_of(c), last_cols], dst_ref=gfull.at[source, rows_of(c), last_cols],
            send_sem=g_send.at[c, o], recv_sem=g_recv.at[c, source],
            device_id={"rep": lax.rem(rep + o, n_rep)}, device_id_type=MESH)

    def early_copy(part, o, source):
        cols = pl.ds(part * 4 * blk, 4 * blk)
        return pltpu.make_async_remote_copy(
            src_ref=grad.at[:, cols], dst_ref=gfull.at[source, :, cols],
            send_sem=gp_send.at[o, part], recv_sem=gp_recv.at[source, part],
            device_id={"rep": lax.rem(rep + o, n_rep)}, device_id_type=MESH)

    def tile_at(j):
        return pl.ds(pl.multiple_of(j * ff_tile, ff_tile), ff_tile)

    def part_copy(c, j, o, source):
        return pltpu.make_async_remote_copy(
            src_ref=masked.at[rep, rows_of(c), tile_at(j)], dst_ref=masked.at[source, rows_of(c), tile_at(j)],
            send_sem=p_send.at[c * n_tiles + j, o], recv_sem=p_recv.at[c * n_tiles + j, source],
            device_id={"rep": lax.rem(rep + o, n_rep)}, device_id_type=MESH)

    def slice_at(s):
        down_at = pl.ds(pl.multiple_of((s // slice_cols) * tall, tall), tall)
        if slice_cols == 1:
            return (down_at,)
        return (down_at, pl.ds(pl.multiple_of((s % slice_cols) * wide, wide), wide))

    def up_rep_copy(o, source):
        return pltpu.make_async_remote_copy(
            src_ref=up.at[slice_at(me)], dst_ref=up_all.at[(source,) + slice_at(me)],
            send_sem=uy_send.at[o], recv_sem=u_recv.at[source, me],
            device_id={"rep": lax.rem(rep + o, n_rep)}, device_id_type=MESH)

    def up_copy(g, s, stage, peer):
        block = up_all.at[(g,) + slice_at(s)]
        return pltpu.make_async_remote_copy(
            src_ref=block, dst_ref=block, send_sem=u_send.at[g, stage], recv_sem=u_recv.at[g, s],
            device_id=peer, device_id_type=MESH)

    def index_of(z, x, core):
        return z * 4 + x * 2 + core

    def along_z(g, z, x, step):
        to = lax.rem(my_z + step + n_z, n_z)
        stage = z * 2 + x
        if step < 0:
            stage = jnp.where(z == my_z, 2 * n_z + x, stage)
        return up_copy(g, index_of(z, x, my_c), stage, z_peer(to))

    def over_x(g):
        return up_copy(g, me, 2 * n_z + 2, x_peer)

    def over_core(g, z, x):
        return up_copy(g, index_of(z, x, my_c), 2 * n_z + 3 + 2 * z + x, core_peer)

    def landed(g, s):
        up_copy(g, s, 0, core_peer).wait_recv()

    for o in range(1, n_rep):
        up_rep_copy(o, rep).start()
    for part in range(z_own - 1):
        for o in range(1, n_rep):
            early_copy(part, o, rep).start()
    for c in range(n_chunks):
        for o in range(1, n_rep):
            grad_copy(c, o, rep).start()
    loads[2].start()
    loads[3].start()
    pl.when(my_z == 0)(lambda: signal(far_sem.at[0], z_peer(my_z + 1)))
    pl.when(my_z == n_z - 1)(lambda: signal(far_sem.at[1], z_peer(my_z - 1)))

    loads[1].wait()
    count = counts[0]

    def mask_rows(c, _):
        at = lax.broadcasted_iota(jnp.int32, (CHUNK, ff), 0) + c * CHUNK
        kept = jnp.where(at < count, hid[rows_of(c), :].astype(jnp.float32), 0.0)
        kept = jnp.maximum(kept, 0.0)
        hid[rows_of(c), :] = kept.astype(jnp.bfloat16)
        return 0

    lax.fori_loop(0, n_chunks, mask_rows, 0)
    loads[0].wait()

    def know_line():
        @pl.when(below)
        def _():
            pl.semaphore_wait(far_sem.at[0], 1)
            pl.when(above)(lambda: signal(far_sem.at[0], z_peer(my_z + 1)))

        @pl.when(above)
        def _():
            pl.semaphore_wait(far_sem.at[1], 1)
            pl.when(below)(lambda: signal(far_sem.at[1], z_peer(my_z - 1)))

    def core_copy(z):
        return pltpu.make_async_remote_copy(
            src_ref=terms.at[z, 1 - my_c], dst_ref=from_core.at[z],
            send_sem=c_send.at[z], recv_sem=c_recv.at[z],
            device_id=core_peer, device_id_type=MESH)

    def x_copy(z):
        return pltpu.make_async_remote_copy(
            src_ref=from_core.at[z, 1 - my_x], dst_ref=from_x.at[z],
            send_sem=x_send.at[z], recv_sem=x_recv.at[z],
            device_id=x_peer, device_id_type=MESH)

    def z_copy(z, source):
        return pltpu.make_async_remote_copy(
            src_ref=from_x.at[z], dst_ref=from_z.at[source],
            send_sem=z_send.at[z], recv_sem=z_recv.at[source],
            device_id=z_peer(z), device_id_type=MESH)

    def z_at(k):
        late = k - z_own
        other = lax.rem(rep + 1 + lax.rem(late, n_rep - 1), n_rep) * z_own + late // (n_rep - 1)
        return jnp.where(k < z_own, rep * z_own + k, other)

    def make_terms(k, _):
        z = z_at(k)
        group = z // z_own
        cols = pl.ds(pl.multiple_of((z - group * z_own) * 4 * blk, 4 * blk), 4 * blk)

        def one(j, _):
            at = tile_at(j)
            out = lax.dot_general(
                gfull[group, :, cols], hid[:, at], (((0,), (0,)), ((), ())),
                preferred_element_type=jnp.float32).astype(jnp.bfloat16)
            for x in range(2):
                for core in range(2):
                    row = (x * 2 + core) * blk
                    terms[z, core, x, :, at] = out[row:row + blk]
            return 0

        lax.fori_loop(0, n_tiles, one, 0)
        core_copy(z).start()
        return 0

    def add_core(k, _):
        z = z_at(k)
        core_copy(z).wait()
        for x in range(2):
            total = from_core[z, x].astype(jnp.float32) + terms[z, my_c, x].astype(jnp.float32)
            from_core[z, x] = total.astype(jnp.bfloat16)
        x_copy(z).start()
        return 0

    def add_x(k, _):
        z = z_at(k)
        x_copy(z).wait()
        total = from_x[z].astype(jnp.float32) + from_core[z, my_x].astype(jnp.float32)
        from_x[z] = total.astype(jnp.bfloat16)

        @pl.when(z != my_z)
        def _():
            z_copy(z, my_z).start()

        return 0

    def chunk(c, _):
        at_rows = rows_of(c)
        for o in range(1, n_rep):
            grad_copy(c, o, lax.rem(rep + o, n_rep)).wait_recv()

        def hidden_tile(j, _):
            at = tile_at(j)
            total = jnp.dot(gfull[0, at_rows, :], down_v[:d_own, at],
                            preferred_element_type=jnp.float32)
            for g in range(1, n_rep):
                total += jnp.dot(gfull[g, at_rows, :], down_v[g * d_own:(g + 1) * d_own, at],
                                 preferred_element_type=jnp.float32)
            passed = hid[at_rows, at].astype(jnp.float32) > 0.0
            masked[rep, at_rows, at] = jnp.where(passed, total, 0.0).astype(jnp.bfloat16)
            for o in range(1, n_rep):
                part_copy(c, j, o, rep).start()
            return 0

        lax.fori_loop(0, n_tiles, hidden_tile, 0)
        return 0

    def start_line(g, x):
        pl.when(above)(lambda: along_z(g, my_z, x, 1).start())
        pl.when(below)(lambda: along_z(g, my_z, x, -1).start())

    def spread_start():
        for g in rep_peers:
            landed(g, me)
            over_x(g).start()
            start_line(g, my_x)
            over_core(g, my_z, my_x).start()

    def spread_x():
        for g in rep_peers:
            landed(g, index_of(my_z, 1 - my_x, my_c))
            start_line(g, 1 - my_x)
            over_core(g, my_z, 1 - my_x).start()

    def spread_z(d, x):
        def visit(z, goes_on, step):
            for g in rep_peers:
                landed(g, index_of(z, x, my_c))
                pl.when(goes_on)(lambda: along_z(g, z, x, step).start())
                over_core(g, z, x).start()

        pl.when(my_z >= d)(lambda: visit(my_z - d, above, 1))
        pl.when(my_z + d < n_z)(lambda: visit(my_z + d, below, -1))

    def spread_rest(d, _):
        spread_z(d, my_x)
        spread_z(d, 1 - my_x)
        return 0

    def spread_end(z, _):
        for g in rep_peers:
            for x in range(2):
                landed(g, index_of(z, x, 1 - my_c))
        return 0

    def spread_sent(z, _):
        for g in rep_peers:
            for x in range(2):
                over_core(g, z, x).wait_send()
                pl.when((z <= my_z) & above)(lambda: along_z(g, z, x, 1).wait_send())
                pl.when((z >= my_z) & below)(lambda: along_z(g, z, x, -1).wait_send())
        return 0

    def finish(c, _):
        at_rows = rows_of(c)

        def arrived(j, _):
            for o in range(1, n_rep):
                part_copy(c, j, o, lax.rem(rep + o, n_rep)).wait_recv()
            return 0

        lax.fori_loop(0, n_tiles, arrived, 0)

        def out_tile(j, _):
            at = pl.ds(pl.multiple_of(j * d_tile, d_tile), d_tile)
            total = jnp.dot(masked[0, at_rows, :], up_all[0, :, at], preferred_element_type=jnp.float32)
            for g in range(1, n_rep):
                total += jnp.dot(masked[g, at_rows, :], up_all[g, :, at], preferred_element_type=jnp.float32)
            ig_out[at_rows, at] = total.astype(jnp.bfloat16)
            return 0

        lax.fori_loop(0, d_all // d_tile, out_tile, 0)
        return 0

    tail = n_chunks - 1
    tail_rows = rows_of(tail)

    def tail_term(g, j, into):
        def one(i, _):
            at = pl.ds(pl.multiple_of(i * d_tile, d_tile), d_tile)
            part = jnp.dot(masked[g, tail_rows, tile_at(j)], up_all[g, tile_at(j), at],
                           preferred_element_type=jnp.float32)

            @pl.when(j == 0)
            def _():
                into[:, at] = part

            @pl.when(j > 0)
            def _():
                into[:, at] += part

            return 0

        lax.fori_loop(0, d_all // d_tile, one, 0)

    def own_tail(j, _):
        tail_term(rep, j, own_sum)
        return 0

    def other_tail(j, _):
        part_copy(tail, j, 1, 1 - rep).wait_recv()
        tail_term(1 - rep, j, other_sum)
        return 0

    first_late, last_late = z_own, n_z - (n_rep - 1)
    third = max(n_chunks // 3, 1)
    lax.fori_loop(0, z_own, make_terms, 0)
    lax.fori_loop(0, 1, add_core, 0)
    spread_start()
    lax.fori_loop(1, z_own, add_core, 0)
    know_line()
    lax.fori_loop(0, 1, add_x, 0)
    spread_z(1, my_x)
    for part in range(z_own - 1):
        for o in range(1, n_rep):
            early_copy(part, o, lax.rem(rep + o, n_rep)).wait_recv()
    lax.fori_loop(first_late, last_late, make_terms, 0)
    spread_x()
    lax.fori_loop(first_late, last_late, add_core, 0)
    loads[2].wait()
    lax.fori_loop(0, third, chunk, 0)
    if n_z > 2:
        spread_z(2, my_x)
    lax.fori_loop(1, z_own, add_x, 0)
    lax.fori_loop(third, 2 * third, chunk, 0)
    spread_z(1, 1 - my_x)
    lax.fori_loop(2 * third, n_chunks, chunk, 0)
    lax.fori_loop(last_late, n_z, make_terms, 0)
    lax.fori_loop(first_late, last_late, add_x, 0)
    lax.fori_loop(last_late, n_z, add_core, 0)
    if n_z > 3:
        spread_z(3, my_x)
    if n_z > 2:
        spread_z(2, 1 - my_x)
    if n_z > 3:
        spread_z(3, 1 - my_x)
    lax.fori_loop(4, n_z, spread_rest, 0)
    loads[3].wait()
    if n_rep == 2:
        lax.fori_loop(0, n_tiles, own_tail, 0)
    lax.fori_loop(last_late, n_z, add_x, 0)
    lax.fori_loop(0, n_z, spread_end, 0)
    lax.fori_loop(0, tail, finish, 0)

    total = from_x[my_z].astype(jnp.float32)
    for o in range(1, n_z):
        source = lax.rem(my_z + o, n_z)
        z_copy(source, source).wait()
        total += from_z[source].astype(jnp.float32)
    dg_out[...] = total / n_dp

    for o in range(1, n_rep):
        for part in range(z_own - 1):
            early_copy(part, o, rep).wait_send()
        up_rep_copy(o, rep).wait_send()
    for g in rep_peers:
        over_x(g).wait_send()
    lax.fori_loop(0, n_z, spread_sent, 0)

    if n_rep == 2:
        lax.fori_loop(0, n_tiles, other_tail, 0)
        ig_out[tail_rows, :] = (own_sum[...] + other_sum[...]).astype(jnp.bfloat16)
    else:
        lax.fori_loop(tail, n_chunks, finish, 0)

    def sent(c, _):
        for o in range(1, n_rep):
            grad_copy(c, o, rep).wait_send()
            for j in range(n_tiles):
                part_copy(c, j, o, rep).wait_send()
        return 0

    lax.fori_loop(0, n_chunks, sent, 0)


def store(n_parts, ig, dg, ig_out, dg_out, sem):
    part = ig.shape[0] // n_parts
    copies = [pltpu.make_async_copy(ig.at[pl.ds(i * part, part)], ig_out.at[pl.ds(i * part, part)], sem.at[i])
              for i in range(n_parts)]
    copies.append(pltpu.make_async_copy(dg, dg_out, sem.at[n_parts]))
    for copy in copies:
        copy.start()
    for copy in copies:
        copy.wait()


def on_device(n_dp, n_rep, grad_out, pre_act, up_weight, down_weight, slot_counts):
    rows, d_own = grad_out.shape
    ff = pre_act.shape[1]
    d_all = down_weight.shape[0]
    n_z = n_dp // 4
    blk = d_all // n_dp
    n_chunks = rows // CHUNK
    n_pieces = n_chunks * (ff // tile_of(ff))
    any_ref = pl.BlockSpec(memory_space=pl.ANY)
    in_vmem = pl.BlockSpec(memory_space=pltpu.VMEM)
    bf16, dma = jnp.bfloat16, pltpu.SemaphoreType.DMA
    results = pl.pallas_call(
        functools.partial(kernel, n_dp, n_rep),
        out_shape=(pltpu.VMEM((rows, d_all), bf16), pltpu.VMEM((blk, ff), jnp.float32)),
        in_specs=[pl.BlockSpec(memory_space=pltpu.SMEM)] + [any_ref] * 4,
        out_specs=(in_vmem,) * 2,
        scratch_shapes=[
            pltpu.VMEM((n_rep, rows, d_own), bf16),
            pltpu.VMEM((rows, ff), bf16),
            pltpu.VMEM((n_rep, ff, d_all), bf16),
            pltpu.VMEM((d_all, ff), bf16),
            pltpu.VMEM((n_z, 2, 2, blk, ff), bf16),
            pltpu.VMEM((n_z, 2, blk, ff), bf16),
            pltpu.VMEM((n_z, blk, ff), bf16),
            pltpu.VMEM((n_z, blk, ff), bf16),
            pltpu.VMEM((n_rep, rows, ff), bf16),
            pltpu.VMEM((CHUNK, d_all), jnp.float32),
            pltpu.VMEM((CHUNK, d_all), jnp.float32),
            pltpu.SemaphoreType.REGULAR((2,)),
            dma((4,)), dma((n_rep, n_z)), dma((n_rep, n_z)),
            dma((n_chunks, n_rep)), dma((n_chunks, n_rep)),
            dma((n_pieces, n_rep)), dma((n_pieces, n_rep)),
            dma((n_rep,)), dma((n_rep, n_dp + 3)), dma((n_rep, n_dp)),
            dma((n_z,)), dma((n_z,)), dma((n_z,)), dma((n_z,)), dma((n_z,)), dma((n_z,)),
        ],
        compiler_params=pltpu.CompilerParams(
            collective_id=0, has_side_effects=True, vmem_limit_bytes=54 * 2**20),
    )(slot_counts, grad_out, pre_act, up_weight, down_weight)
    n_parts = 4
    return pl.pallas_call(
        functools.partial(store, n_parts),
        out_shape=(jax.ShapeDtypeStruct((rows, d_all), bf16), jax.ShapeDtypeStruct((blk, ff), jnp.float32)),
        in_specs=[in_vmem] * 2,
        out_specs=(any_ref,) * 2,
        scratch_shapes=[dma((n_parts + 1,))],
        compiler_params=pltpu.CompilerParams(vmem_limit_bytes=6 * 2**20),
    )(*results)


def solution(mesh):
    sizes = dict(mesh.shape)
    return jax.shard_map(
        functools.partial(on_device, sizes["dp"], sizes["rep"]),
        mesh=mesh,
        in_specs=(P("dp", "rep"), P("dp", "rep"), P("rep", None), P(None, "rep"), P("dp")),
        out_specs=(P("dp", None), P("dp", "rep")),
        check_vma=False,
    )
```

```python
import functools

import jax
import jax.numpy as jnp
from jax import lax
from jax.experimental import pallas as pl
from jax.experimental.pallas import tpu as pltpu
from jax.sharding import PartitionSpec as P

MESH = pl.DeviceIdType.MESH
CHUNK = 128


def tile_of(extent):
    return next(t for t in (512, 384, 256, 128) if extent % t == 0)


def piece_of(extent):
    return next(t for t in (256, 128) if extent % t == 0)


def kernel(n_dp, n_rep, counts, grad, pre, up, down, ig_out, dg_out,
           gfull, hid, up_all, down_v, terms, from_core, from_x, from_z, masked, own_sum, other_sum,
           far_sem, load_sem, gp_send, gp_recv, g_send, g_recv, p_send, p_recv, t_recv, uy_send, uz_send, ux_send,
           uc_send, u_recv, uc_recv, c_send, c_recv, x_send, x_recv, z_send, z_recv):
    rows, d_own = grad.shape
    ff = pre.shape[1]
    d_all = down.shape[0]
    n_z = n_dp // 4
    z_own = n_z // n_rep
    blk = d_all // n_dp
    n_chunks = rows // CHUNK
    ff_tile, d_tile = tile_of(ff), tile_of(d_all)
    n_tiles = ff // ff_tile
    piece = piece_of(ff)
    n_pieces = ff // piece
    slice_rows = n_dp
    while ff % (slice_rows * 16):
        slice_rows //= 2
    slice_cols = n_dp // slice_rows
    tall, wide = ff // slice_rows, d_all // slice_cols

    me = lax.axis_index("dp")
    rep = lax.axis_index("rep")
    my_z, my_x, my_c = me // 4, (me // 2) % 2, me % 2
    core_peer = {"dp": my_z * 4 + my_x * 2 + (1 - my_c)}
    x_peer = {"dp": my_z * 4 + (1 - my_x) * 2 + my_c}
    offsets = range(1, n_rep)
    above, below = my_z + 1 < n_z, my_z > 0

    def ahead(o):
        return lax.rem(rep + o, n_rep)

    def behind(o):
        return lax.rem(rep + n_rep - o, n_rep)

    def send(src, dst, send_sem, recv_sem, peer):
        return pltpu.make_async_remote_copy(src_ref=src, dst_ref=dst, send_sem=send_sem, recv_sem=recv_sem,
                                            device_id=peer, device_id_type=MESH)

    def all_of(ref, sem):
        pltpu.make_async_copy(ref, ref, sem).wait()

    def z_peer(z):
        return {"dp": z * 4 + my_x * 2 + my_c}

    def signal(sem, peer):
        pl.semaphore_signal(sem, inc=1, device_id=peer, device_id_type=MESH)

    barrier = pltpu.get_barrier_semaphore()
    near = [{"rep": ahead(o)} for o in offsets] + [core_peer, x_peer]
    for peer in near:
        signal(barrier, peer)
    pl.when(above)(lambda: signal(barrier, z_peer(my_z + 1)))
    pl.when(below)(lambda: signal(barrier, z_peer(my_z - 1)))

    loads = [
        pltpu.make_async_copy(src, dst, load_sem.at[i])
        for i, (src, dst) in enumerate(
            ((grad, gfull.at[rep]), (pre, hid), (down, down_v), (up, up_all.at[rep])))
    ]
    loads[1].start()
    loads[0].start()
    pl.semaphore_wait(barrier, len(near) + above.astype(jnp.int32) + below.astype(jnp.int32))

    def rows_of(c):
        return pl.ds(pl.multiple_of(c * CHUNK, CHUNK), CHUNK)

    last_cols = pl.ds((z_own - 1) * 4 * blk, 4 * blk)

    def grad_copy(c, o, source):
        return send(grad.at[rows_of(c), last_cols], gfull.at[source, rows_of(c), last_cols],
                    g_send.at[o - 1], g_recv.at[c, o - 1], {"rep": ahead(o)})

    def early_copy(part, o, source):
        cols = pl.ds(part * 4 * blk, 4 * blk)
        return send(grad.at[:, cols], gfull.at[source, :, cols],
                    gp_send.at[part, o - 1], gp_recv.at[part, o - 1], {"rep": ahead(o)})

    def tile_at(j):
        return pl.ds(pl.multiple_of(j * ff_tile, ff_tile), ff_tile)

    def piece_at(j):
        return pl.ds(pl.multiple_of(j * piece, piece), piece)

    def part_copy(c, j, o):
        block = masked.at[rep, rows_of(c), tile_at(j)]
        return send(block, block, p_send.at[o - 1], p_recv.at[c, o - 1], {"rep": ahead(o)})

    def tail_copy(j, o):
        block = masked.at[rep, tail_rows, piece_at(j)]
        return send(block, block, p_send.at[o - 1], t_recv.at[j, o - 1], {"rep": ahead(o)})

    def tail_arrived(j, o):
        all_of(masked.at[behind(o), tail_rows, piece_at(j)], t_recv.at[j, o - 1])

    def slice_at(s):
        down_at = pl.ds(pl.multiple_of((s // slice_cols) * tall, tall), tall)
        if slice_cols == 1:
            return (down_at,)
        return (down_at, pl.ds(pl.multiple_of((s % slice_cols) * wide, wide), wide))

    def index_of(z, x, core):
        return z * 4 + x * 2 + core

    def up_rep_copy(o):
        return send(up.at[slice_at(me)], up_all.at[(rep,) + slice_at(me)],
                    uy_send.at[o - 1], u_recv.at[my_z * 2 + my_x, o - 1], {"rep": ahead(o)})

    def up_copy(o, s, send_sem, peer):
        block = up_all.at[(behind(o),) + slice_at(s)]
        return send(block, block, send_sem, u_recv.at[s // 2, o - 1], peer)

    def along_z(o, z, step):
        to = lax.rem(my_z + step + n_z, n_z)
        stage = z if step > 0 else jnp.where(z == my_z, n_z, z)
        return up_copy(o, index_of(z, my_x, my_c), uz_send.at[stage, o - 1], z_peer(to))

    def over_x(o, z):
        return up_copy(o, index_of(z, my_x, my_c), ux_send.at[o - 1], x_peer)

    def over_core(o, z, x):
        block = up_all.at[(behind(o),) + slice_at(index_of(z, x, my_c))]
        return send(block, block, uc_send.at[o - 1], uc_recv.at[o - 1], core_peer)

    def landed(o, z, x):
        up_copy(o, index_of(z, x, my_c), ux_send.at[o - 1], x_peer).wait_recv()

    for o in offsets:
        up_rep_copy(o).start()
    for part in range(z_own - 1):
        for o in offsets:
            early_copy(part, o, rep).start()
    for c in range(n_chunks):
        for o in offsets:
            grad_copy(c, o, rep).start()
    pl.when(my_z == 0)(lambda: signal(far_sem.at[0], z_peer(my_z + 1)))
    pl.when(my_z == n_z - 1)(lambda: signal(far_sem.at[1], z_peer(my_z - 1)))

    loads[1].wait()
    count = counts[0]

    def mask_rows(c, _):
        at = lax.broadcasted_iota(jnp.int32, (CHUNK, ff), 0) + c * CHUNK
        kept = jnp.where(at < count, hid[rows_of(c), :].astype(jnp.float32), 0.0)
        kept = jnp.maximum(kept, 0.0)
        hid[rows_of(c), :] = kept.astype(jnp.bfloat16)
        return 0

    lax.fori_loop(0, n_chunks, mask_rows, 0)
    loads[0].wait()

    def know_line():
        @pl.when(below)
        def _():
            pl.semaphore_wait(far_sem.at[0], 1)
            pl.when(above)(lambda: signal(far_sem.at[0], z_peer(my_z + 1)))

        @pl.when(above)
        def _():
            pl.semaphore_wait(far_sem.at[1], 1)
            pl.when(below)(lambda: signal(far_sem.at[1], z_peer(my_z - 1)))

    def core_copy(z):
        return send(terms.at[z, 1 - my_c], from_core.at[z], c_send, c_recv.at[z], core_peer)

    def x_copy(z):
        return send(from_core.at[z, 1 - my_x], from_x.at[z], x_send, x_recv.at[z], x_peer)

    def z_copy(z, source):
        slot = jnp.where(source > z, source - 1, source)
        return send(from_x.at[z], from_z.at[slot], z_send, z_recv, z_peer(z))

    def z_at(k):
        late = k - z_own
        other = lax.rem(rep + 1 + lax.rem(late, n_rep - 1), n_rep) * z_own + late // (n_rep - 1)
        return jnp.where(k < z_own, rep * z_own + k, other)

    def make_terms(k, _):
        z = z_at(k)
        group = z // z_own
        cols = pl.ds(pl.multiple_of((z - group * z_own) * 4 * blk, 4 * blk), 4 * blk)

        def one(j, _):
            at = tile_at(j)
            out = lax.dot_general(
                gfull[group, :, cols], hid[:, at], (((0,), (0,)), ((), ())),
                preferred_element_type=jnp.float32).astype(jnp.bfloat16)
            for x in range(2):
                for core in range(2):
                    row = (x * 2 + core) * blk
                    terms[z, core, x, :, at] = out[row:row + blk]
            return 0

        lax.fori_loop(0, n_tiles, one, 0)
        core_copy(z).start()
        return 0

    def add_core(k, _):
        z = z_at(k)
        core_copy(z).wait_recv()
        for x in range(2):
            total = from_core[z, x].astype(jnp.float32) + terms[z, my_c, x].astype(jnp.float32)
            from_core[z, x] = total.astype(jnp.bfloat16)
        x_copy(z).start()
        return 0

    def add_x(k, _):
        z = z_at(k)
        x_copy(z).wait_recv()
        total = from_x[z].astype(jnp.float32) + from_core[z, my_x].astype(jnp.float32)
        from_x[z] = total.astype(jnp.bfloat16)

        @pl.when(z != my_z)
        def _():
            z_copy(z, my_z).start()

        return 0

    tail = n_chunks - 1
    tail_rows = rows_of(tail)

    def hidden_part(at_rows, at):
        total = jnp.dot(gfull[0, at_rows, :], down_v[:d_own, at], preferred_element_type=jnp.float32)
        for g in range(1, n_rep):
            total += jnp.dot(gfull[g, at_rows, :], down_v[g * d_own:(g + 1) * d_own, at],
                             preferred_element_type=jnp.float32)
        passed = hid[at_rows, at].astype(jnp.float32) > 0.0
        masked[rep, at_rows, at] = jnp.where(passed, total, 0.0).astype(jnp.bfloat16)

    def grads_arrived(c):
        for o in offsets:
            grad_copy(c, o, behind(o)).wait_recv()

    def chunk(c, _):
        grads_arrived(c)

        def hidden_tile(j, _):
            hidden_part(rows_of(c), tile_at(j))
            for o in offsets:
                part_copy(c, j, o).start()
            return 0

        lax.fori_loop(0, n_tiles, hidden_tile, 0)
        return 0

    def tail_chunk():
        grads_arrived(tail)

        def hidden_piece(j, _):
            hidden_part(tail_rows, piece_at(j))
            for o in offsets:
                tail_copy(j, o).start()
            return 0

        lax.fori_loop(0, n_pieces, hidden_piece, 0)

    def own_part(c, _):
        def own_tile(j, _):
            at = pl.ds(pl.multiple_of(j * d_tile, d_tile), d_tile)
            own_sum[rows_of(c), at] = jnp.dot(masked[rep, rows_of(c), :], up_all[rep, :, at],
                                              preferred_element_type=jnp.float32)
            return 0

        lax.fori_loop(0, d_all // d_tile, own_tile, 0)
        return 0

    def spread_start():
        for o in offsets:
            landed(o, my_z, my_x)
            pl.when(above)(lambda: along_z(o, my_z, 1).start())
            pl.when(below)(lambda: along_z(o, my_z, -1).start())
            over_x(o, my_z).start()
            over_core(o, my_z, my_x).start()

    def both_sides(d, visit):
        pl.when(my_z >= d)(lambda: visit(my_z - d, above, 1))
        pl.when(my_z + d < n_z)(lambda: visit(my_z + d, below, -1))

    def spread_z(d, _):
        def visit(z, goes_on, step):
            for o in offsets:
                landed(o, z, my_x)
                pl.when(goes_on)(lambda: along_z(o, z, step).start())
                over_core(o, z, my_x).start()

        both_sides(d, visit)
        return 0

    def cross_x(d, _):
        def visit(z, goes_on, step):
            for o in offsets:
                over_x(o, z).start()

        both_sides(d, visit)
        return 0

    def pass_core(z):
        for o in offsets:
            landed(o, z, 1 - my_x)
            over_core(o, z, 1 - my_x).start()

    def spread_core(d, _):
        both_sides(d, lambda z, goes_on, step: pass_core(z))
        return 0

    def spread_sent(z, _):
        for o in offsets:
            pl.when((z <= my_z) & above)(lambda: along_z(o, z, 1).wait_send())
            pl.when((z >= my_z) & below)(lambda: along_z(o, z, -1).wait_send())
        return 0

    def finish(c, _):
        at_rows = rows_of(c)
        for o in offsets:
            all_of(masked.at[behind(o), at_rows], p_recv.at[c, o - 1])

        def out_tile(j, _):
            at = pl.ds(pl.multiple_of(j * d_tile, d_tile), d_tile)

            def term(g):
                return jnp.dot(masked[g, at_rows, :], up_all[g, :, at], preferred_element_type=jnp.float32)

            if n_rep == 2:
                total = own_sum[at_rows, at] + term(1 - rep)
            else:
                total = sum_terms(term)
            ig_out[at_rows, at] = total.astype(jnp.bfloat16)
            return 0

        lax.fori_loop(0, d_all // d_tile, out_tile, 0)
        return 0

    def sum_terms(term):
        total = term(0)
        for g in range(1, n_rep):
            total += term(g)
        return total

    def tail_term(g, j, at):
        return jnp.dot(masked[g, tail_rows, piece_at(j)], up_all[g, piece_at(j), at],
                       preferred_element_type=jnp.float32)

    def tail_tiles(visit):
        def one(i, _):
            visit(pl.ds(pl.multiple_of(i * d_tile, d_tile), d_tile))
            return 0

        lax.fori_loop(0, d_all // d_tile, one, 0)

    def tail_first(g, ref, rows_at):
        def visit(at):
            ref[rows_at, at] = tail_term(g, 0, at)

        tail_tiles(visit)

    def tail_add(g, j, ref, rows_at):
        def visit(at):
            ref[rows_at, at] += tail_term(g, j, at)

        tail_tiles(visit)

    def tail_last(g, j):
        def visit(at):
            other = tail_term(g, j, at)
            if n_pieces > 1:
                other = other_sum[:, at] + other
            ig_out[tail_rows, at] = (own_sum[tail_rows, at] + other).astype(jnp.bfloat16)

        tail_tiles(visit)

    def own_tail():
        tail_first(rep, own_sum, tail_rows)

        def step(j, _):
            tail_add(rep, j, own_sum, tail_rows)
            return 0

        lax.fori_loop(1, n_pieces, step, 0)

    def other_tail():
        everything = pl.ds(0, CHUNK)
        if n_pieces > 1:
            tail_arrived(0, 1)
            tail_first(1 - rep, other_sum, everything)

            def step(j, _):
                tail_arrived(j, 1)
                tail_add(1 - rep, j, other_sum, everything)
                return 0

            lax.fori_loop(1, n_pieces - 1, step, 0)
        tail_arrived(n_pieces - 1, 1)
        tail_last(1 - rep, n_pieces - 1)

    def finish_tail():
        for o in offsets:
            for j in range(n_pieces):
                tail_arrived(j, o)

        def visit(at):
            total = sum_terms(lambda g: jnp.dot(masked[g, tail_rows, :], up_all[g, :, at],
                                                preferred_element_type=jnp.float32))
            ig_out[tail_rows, at] = total.astype(jnp.bfloat16)

        tail_tiles(visit)

    first_late, last_late = z_own, n_z - (n_rep - 1)
    third = max(n_chunks // 3, 1)
    lax.fori_loop(0, z_own, make_terms, 0)
    lax.fori_loop(0, z_own, add_core, 0)
    loads[2].start()
    spread_start()
    loads[3].start()
    know_line()
    lax.fori_loop(1, 2, spread_z, 0)
    for part in range(z_own - 1):
        for o in offsets:
            early_copy(part, o, behind(o)).wait_recv()
    lax.fori_loop(first_late, last_late, make_terms, 0)
    lax.fori_loop(first_late, last_late, add_core, 0)
    lax.fori_loop(1, 2, cross_x, 0)
    lax.fori_loop(2, min(3, n_z), spread_z, 0)
    lax.fori_loop(0, 1, add_x, 0)
    loads[2].wait()
    lax.fori_loop(0, third, chunk, 0)
    lax.fori_loop(1, z_own, add_x, 0)
    lax.fori_loop(third, 2 * third, chunk, 0)
    pass_core(my_z)
    lax.fori_loop(2 * third, tail, chunk, 0)
    tail_chunk()
    lax.fori_loop(3, n_z, spread_z, 0)
    lax.fori_loop(last_late, n_z, make_terms, 0)
    lax.fori_loop(last_late, n_z, add_core, 0)
    lax.fori_loop(2, n_z, cross_x, 0)
    lax.fori_loop(first_late, last_late, add_x, 0)
    loads[3].wait()
    if n_rep == 2:
        lax.fori_loop(0, tail, own_part, 0)
        own_tail()
    lax.fori_loop(1, 2, spread_core, 0)
    lax.fori_loop(last_late, n_z, add_x, 0)
    lax.fori_loop(2, n_z, spread_core, 0)
    for o in offsets:
        all_of(up_all.at[behind(o), pl.ds(0, ff // 2)], uc_recv.at[o - 1])
    lax.fori_loop(0, tail, finish, 0)

    total = from_x[my_z].astype(jnp.float32)
    all_of(from_z, z_recv)
    for o in range(n_z - 1):
        total += from_z[o].astype(jnp.float32)
    dg_out[...] = total / n_dp

    for o in offsets:
        for part in range(z_own - 1):
            early_copy(part, o, rep).wait_send()
        all_of(grad.at[:, last_cols], g_send.at[o - 1])
        up_rep_copy(o).wait_send()
        all_of(up_all.at[behind(o), pl.ds(0, ff // 2)], uc_send.at[o - 1])
        all_of(up_all.at[behind(o), pl.ds(0, ff // 4)], ux_send.at[o - 1])
    lax.fori_loop(0, n_z, spread_sent, 0)
    all_of(from_core, c_send)
    all_of(from_x, x_send)
    all_of(from_z, z_send)

    if n_rep == 2:
        other_tail()
    else:
        finish_tail()
    for o in offsets:
        all_of(masked.at[rep], p_send.at[o - 1])


def store(n_parts, ig, dg, ig_out, dg_out, sem):
    part = ig.shape[0] // n_parts
    copies = [pltpu.make_async_copy(ig.at[pl.ds(i * part, part)], ig_out.at[pl.ds(i * part, part)], sem.at[i])
              for i in range(n_parts)]
    copies.append(pltpu.make_async_copy(dg, dg_out, sem.at[n_parts]))
    for copy in copies:
        copy.start()
    for copy in copies:
        copy.wait()


def on_device(n_dp, n_rep, grad_out, pre_act, up_weight, down_weight, slot_counts):
    rows, d_own = grad_out.shape
    ff = pre_act.shape[1]
    d_all = down_weight.shape[0]
    n_z = n_dp // 4
    blk = d_all // n_dp
    n_chunks = rows // CHUNK
    n_pieces = ff // piece_of(ff)
    z_own, others = n_z // n_rep, n_rep - 1
    any_ref = pl.BlockSpec(memory_space=pl.ANY)
    in_vmem = pl.BlockSpec(memory_space=pltpu.VMEM)
    bf16, dma = jnp.bfloat16, pltpu.SemaphoreType.DMA
    results = pl.pallas_call(
        functools.partial(kernel, n_dp, n_rep),
        out_shape=(pltpu.VMEM((rows, d_all), bf16), pltpu.VMEM((blk, ff), jnp.float32)),
        in_specs=[pl.BlockSpec(memory_space=pltpu.SMEM)] + [any_ref] * 4,
        out_specs=(in_vmem,) * 2,
        scratch_shapes=[
            pltpu.VMEM((n_rep, rows, d_own), bf16),
            pltpu.VMEM((rows, ff), bf16),
            pltpu.VMEM((n_rep, ff, d_all), bf16),
            pltpu.VMEM((d_all, ff), bf16),
            pltpu.VMEM((n_z, 2, 2, blk, ff), bf16),
            pltpu.VMEM((n_z, 2, blk, ff), bf16),
            pltpu.VMEM((n_z, blk, ff), bf16),
            pltpu.VMEM((n_z - 1, blk, ff), bf16),
            pltpu.VMEM((n_rep, rows, ff), bf16),
            pltpu.VMEM((rows, d_all), jnp.float32),
            pltpu.VMEM((CHUNK, d_all), jnp.float32),
            pltpu.SemaphoreType.REGULAR((2,)),
            dma((4,)), dma((max(z_own - 1, 1), others)), dma((max(z_own - 1, 1), others)),
            dma((others,)), dma((n_chunks, others)),
            dma((others,)), dma((n_chunks - 1, others)), dma((n_pieces, others)),
            dma((others,)), dma((n_z + 1, others)), dma((others,)), dma((others,)),
            dma((2 * n_z, others)), dma((others,)),
            dma, dma((n_z,)), dma, dma((n_z,)), dma, dma,
        ],
        compiler_params=pltpu.CompilerParams(
            collective_id=0, has_side_effects=True, vmem_limit_bytes=56 * 2**20),
    )(slot_counts, grad_out, pre_act, up_weight, down_weight)
    n_parts = 4
    return pl.pallas_call(
        functools.partial(store, n_parts),
        out_shape=(jax.ShapeDtypeStruct((rows, d_all), bf16), jax.ShapeDtypeStruct((blk, ff), jnp.float32)),
        in_specs=[in_vmem] * 2,
        out_specs=(any_ref,) * 2,
        scratch_shapes=[dma((n_parts + 1,))],
        compiler_params=pltpu.CompilerParams(vmem_limit_bytes=6 * 2**20),
    )(*results)


def solution(mesh):
    sizes = dict(mesh.shape)
    return jax.shard_map(
        functools.partial(on_device, sizes["dp"], sizes["rep"]),
        mesh=mesh,
        in_specs=(P("dp", "rep"), P("dp", "rep"), P("rep", None), P(None, "rep"), P("dp")),
        out_specs=(P("dp", None), P("dp", "rep")),
        check_vma=False,
    )
```

```python
import functools

import jax
import jax.numpy as jnp
from jax import lax
from jax.experimental import pallas as pl
from jax.experimental.pallas import tpu as pltpu
from jax.sharding import PartitionSpec as P

MESH = pl.DeviceIdType.MESH
CHUNK = 128


def tile_of(extent):
    return next(t for t in (512, 384, 256, 128) if extent % t == 0)


def piece_of(extent):
    return next(t for t in (256, 128) if extent % t == 0)


def kernel(n_dp, n_rep, counts, grad, pre, up, down, ig_out, dg_out,
           gfull, hid, up_all, down_v, terms, from_core, from_x, from_z, masked, own_sum, other_sum,
           far_sem, load_sem, gp_send, gp_recv, g_send, g_recv, p_send, p_recv, t_recv, uy_send, uz_send, ux_send,
           uc_send, u_recv, uc_recv, c_send, c_recv, x_send, x_recv, z_send, z_recv):
    rows, d_own = grad.shape
    ff = pre.shape[1]
    d_all = down.shape[0]
    n_z = n_dp // 4
    z_own = n_z // n_rep
    blk = d_all // n_dp
    n_chunks = rows // CHUNK
    ff_tile, d_tile = tile_of(ff), tile_of(d_all)
    n_tiles = ff // ff_tile
    piece = piece_of(ff)
    n_pieces = ff // piece
    slice_rows = n_dp
    while ff % (slice_rows * 16):
        slice_rows //= 2
    slice_cols = n_dp // slice_rows
    tall, wide = ff // slice_rows, d_all // slice_cols

    me = lax.axis_index("dp")
    rep = lax.axis_index("rep")
    my_z, my_x, my_c = me // 4, (me // 2) % 2, me % 2
    core_peer = {"dp": my_z * 4 + my_x * 2 + (1 - my_c)}
    x_peer = {"dp": my_z * 4 + (1 - my_x) * 2 + my_c}
    offsets = range(1, n_rep)
    above, below = my_z + 1 < n_z, my_z > 0

    def ahead(o):
        return lax.rem(rep + o, n_rep)

    def behind(o):
        return lax.rem(rep + n_rep - o, n_rep)

    def send(src, dst, send_sem, recv_sem, peer):
        return pltpu.make_async_remote_copy(src_ref=src, dst_ref=dst, send_sem=send_sem, recv_sem=recv_sem,
                                            device_id=peer, device_id_type=MESH)

    def all_of(ref, sem):
        pltpu.make_async_copy(ref, ref, sem).wait()

    def z_peer(z):
        return {"dp": z * 4 + my_x * 2 + my_c}

    def signal(sem, peer):
        pl.semaphore_signal(sem, inc=1, device_id=peer, device_id_type=MESH)

    barrier = pltpu.get_barrier_semaphore()
    near = [{"rep": ahead(o)} for o in offsets] + [core_peer, x_peer]
    for peer in near:
        signal(barrier, peer)
    pl.when(above)(lambda: signal(barrier, z_peer(my_z + 1)))
    pl.when(below)(lambda: signal(barrier, z_peer(my_z - 1)))

    loads = [
        pltpu.make_async_copy(src, dst, load_sem.at[i])
        for i, (src, dst) in enumerate(
            ((grad, gfull.at[rep]), (pre, hid), (down, down_v), (up, up_all.at[rep])))
    ]
    loads[0].start()
    loads[1].start()
    pl.semaphore_wait(barrier, len(near) + above.astype(jnp.int32) + below.astype(jnp.int32))

    def rows_of(c):
        return pl.ds(pl.multiple_of(c * CHUNK, CHUNK), CHUNK)

    last_cols = pl.ds((z_own - 1) * 4 * blk, 4 * blk)

    def grad_copy(c, o, source):
        return send(gfull.at[rep, rows_of(c), last_cols], gfull.at[source, rows_of(c), last_cols],
                    g_send.at[o - 1], g_recv.at[c, o - 1], {"rep": ahead(o)})

    def early_copy(part, o, source):
        cols = pl.ds(part * 4 * blk, 4 * blk)
        return send(gfull.at[rep, :, cols], gfull.at[source, :, cols],
                    gp_send.at[part, o - 1], gp_recv.at[part, o - 1], {"rep": ahead(o)})

    def tile_at(j):
        return pl.ds(pl.multiple_of(j * ff_tile, ff_tile), ff_tile)

    def piece_at(j):
        return pl.ds(pl.multiple_of(j * piece, piece), piece)

    def part_copy(c, j, o):
        block = masked.at[rep, rows_of(c), tile_at(j)]
        return send(block, block, p_send.at[o - 1], p_recv.at[c, o - 1], {"rep": ahead(o)})

    def tail_copy(j, o):
        block = masked.at[rep, tail_rows, piece_at(j)]
        return send(block, block, p_send.at[o - 1], t_recv.at[j, o - 1], {"rep": ahead(o)})

    def tail_arrived(j, o):
        all_of(masked.at[behind(o), tail_rows, piece_at(j)], t_recv.at[j, o - 1])

    def slice_at(s):
        down_at = pl.ds(pl.multiple_of((s // slice_cols) * tall, tall), tall)
        if slice_cols == 1:
            return (down_at,)
        return (down_at, pl.ds(pl.multiple_of((s % slice_cols) * wide, wide), wide))

    def index_of(z, x, core):
        return z * 4 + x * 2 + core

    def up_rep_copy(o):
        return send(up.at[slice_at(me)], up_all.at[(rep,) + slice_at(me)],
                    uy_send.at[o - 1], u_recv.at[my_z * 2 + my_x, o - 1], {"rep": ahead(o)})

    def up_copy(o, s, send_sem, peer):
        block = up_all.at[(behind(o),) + slice_at(s)]
        return send(block, block, send_sem, u_recv.at[s // 2, o - 1], peer)

    def along_z(o, z, step):
        to = lax.rem(my_z + step + n_z, n_z)
        stage = z if step > 0 else jnp.where(z == my_z, n_z, z)
        return up_copy(o, index_of(z, my_x, my_c), uz_send.at[stage, o - 1], z_peer(to))

    def over_x(o, z):
        return up_copy(o, index_of(z, my_x, my_c), ux_send.at[o - 1], x_peer)

    def over_core(o, z, x):
        block = up_all.at[(behind(o),) + slice_at(index_of(z, x, my_c))]
        return send(block, block, uc_send.at[o - 1], uc_recv.at[o - 1], core_peer)

    def landed(o, z, x):
        up_copy(o, index_of(z, x, my_c), ux_send.at[o - 1], x_peer).wait_recv()

    for o in offsets:
        up_rep_copy(o).start()
    loads[0].wait()
    for part in range(z_own - 1):
        for o in offsets:
            early_copy(part, o, rep).start()
    for c in range(n_chunks):
        for o in offsets:
            grad_copy(c, o, rep).start()
    pl.when(my_z == 0)(lambda: signal(far_sem.at[0], z_peer(my_z + 1)))
    pl.when(my_z == n_z - 1)(lambda: signal(far_sem.at[1], z_peer(my_z - 1)))

    loads[1].wait()
    count = counts[0]

    def mask_rows(c, _):
        at = lax.broadcasted_iota(jnp.int32, (CHUNK, ff), 0) + c * CHUNK
        kept = jnp.where(at < count, hid[rows_of(c), :].astype(jnp.float32), 0.0)
        kept = jnp.maximum(kept, 0.0)
        hid[rows_of(c), :] = kept.astype(jnp.bfloat16)
        return 0

    lax.fori_loop(0, n_chunks, mask_rows, 0)

    def know_line():
        @pl.when(below)
        def _():
            pl.semaphore_wait(far_sem.at[0], 1)
            pl.when(above)(lambda: signal(far_sem.at[0], z_peer(my_z + 1)))

        @pl.when(above)
        def _():
            pl.semaphore_wait(far_sem.at[1], 1)
            pl.when(below)(lambda: signal(far_sem.at[1], z_peer(my_z - 1)))

    def core_copy(z):
        return send(terms.at[z, 1 - my_c], from_core.at[z], c_send, c_recv.at[z], core_peer)

    def x_copy(z):
        return send(from_core.at[z, 1 - my_x], from_x.at[z], x_send, x_recv.at[z], x_peer)

    def z_copy(z, source):
        slot = jnp.where(source > z, source - 1, source)
        return send(from_x.at[z], from_z.at[slot], z_send, z_recv, z_peer(z))

    def z_at(k):
        late = k - z_own
        other = lax.rem(rep + 1 + lax.rem(late, n_rep - 1), n_rep) * z_own + late // (n_rep - 1)
        return jnp.where(k < z_own, rep * z_own + k, other)

    def make_terms(k, _):
        z = z_at(k)
        group = z // z_own
        cols = pl.ds(pl.multiple_of((z - group * z_own) * 4 * blk, 4 * blk), 4 * blk)

        def one(j, _):
            at = tile_at(j)
            out = lax.dot_general(
                gfull[group, :, cols], hid[:, at], (((0,), (0,)), ((), ())),
                preferred_element_type=jnp.float32).astype(jnp.bfloat16)
            for x in range(2):
                for core in range(2):
                    row = (x * 2 + core) * blk
                    terms[z, core, x, :, at] = out[row:row + blk]
            return 0

        lax.fori_loop(0, n_tiles, one, 0)
        core_copy(z).start()
        return 0

    def add_core(k, _):
        z = z_at(k)
        core_copy(z).wait_recv()
        for x in range(2):
            total = from_core[z, x].astype(jnp.float32) + terms[z, my_c, x].astype(jnp.float32)
            from_core[z, x] = total.astype(jnp.bfloat16)
        x_copy(z).start()
        return 0

    def add_x(k, _):
        z = z_at(k)
        x_copy(z).wait_recv()
        total = from_x[z].astype(jnp.float32) + from_core[z, my_x].astype(jnp.float32)
        from_x[z] = total.astype(jnp.bfloat16)

        @pl.when(z != my_z)
        def _():
            z_copy(z, my_z).start()

        return 0

    tail = n_chunks - 1
    tail_rows = rows_of(tail)

    def hidden_part(at_rows, at):
        total = jnp.dot(gfull[0, at_rows, :], down_v[:d_own, at], preferred_element_type=jnp.float32)
        for g in range(1, n_rep):
            total += jnp.dot(gfull[g, at_rows, :], down_v[g * d_own:(g + 1) * d_own, at],
                             preferred_element_type=jnp.float32)
        passed = hid[at_rows, at].astype(jnp.float32) > 0.0
        masked[rep, at_rows, at] = jnp.where(passed, total, 0.0).astype(jnp.bfloat16)

    def grads_arrived(c):
        for o in offsets:
            grad_copy(c, o, behind(o)).wait_recv()

    def chunk(c, _):
        grads_arrived(c)

        def hidden_tile(j, _):
            hidden_part(rows_of(c), tile_at(j))
            for o in offsets:
                part_copy(c, j, o).start()
            return 0

        lax.fori_loop(0, n_tiles, hidden_tile, 0)
        return 0

    def tail_chunk():
        grads_arrived(tail)

        def hidden_piece(j, _):
            hidden_part(tail_rows, piece_at(j))
            for o in offsets:
                tail_copy(j, o).start()
            return 0

        lax.fori_loop(0, n_pieces, hidden_piece, 0)

    def own_part(c, _):
        def own_tile(j, _):
            at = pl.ds(pl.multiple_of(j * d_tile, d_tile), d_tile)
            own_sum[rows_of(c), at] = jnp.dot(masked[rep, rows_of(c), :], up_all[rep, :, at],
                                              preferred_element_type=jnp.float32)
            return 0

        lax.fori_loop(0, d_all // d_tile, own_tile, 0)
        return 0

    def spread_start():
        for o in offsets:
            landed(o, my_z, my_x)
            pl.when(above)(lambda: along_z(o, my_z, 1).start())
            pl.when(below)(lambda: along_z(o, my_z, -1).start())
            over_x(o, my_z).start()
            over_core(o, my_z, my_x).start()

    def both_sides(d, visit):
        pl.when(my_z >= d)(lambda: visit(my_z - d, above, 1))
        pl.when(my_z + d < n_z)(lambda: visit(my_z + d, below, -1))

    def spread_z(d, _):
        def visit(z, goes_on, step):
            for o in offsets:
                landed(o, z, my_x)
                pl.when(goes_on)(lambda: along_z(o, z, step).start())
                over_core(o, z, my_x).start()

        both_sides(d, visit)
        return 0

    def cross_x(d, _):
        def visit(z, goes_on, step):
            for o in offsets:
                over_x(o, z).start()

        both_sides(d, visit)
        return 0

    def pass_core(z):
        for o in offsets:
            landed(o, z, 1 - my_x)
            over_core(o, z, 1 - my_x).start()

    def spread_core(d, _):
        both_sides(d, lambda z, goes_on, step: pass_core(z))
        return 0

    def spread_sent(z, _):
        for o in offsets:
            pl.when((z <= my_z) & above)(lambda: along_z(o, z, 1).wait_send())
            pl.when((z >= my_z) & below)(lambda: along_z(o, z, -1).wait_send())
        return 0

    def finish(c, _):
        at_rows = rows_of(c)
        for o in offsets:
            all_of(masked.at[behind(o), at_rows], p_recv.at[c, o - 1])

        def out_tile(j, _):
            at = pl.ds(pl.multiple_of(j * d_tile, d_tile), d_tile)

            def term(g):
                return jnp.dot(masked[g, at_rows, :], up_all[g, :, at], preferred_element_type=jnp.float32)

            if n_rep == 2:
                total = own_sum[at_rows, at] + term(1 - rep)
            else:
                total = sum_terms(term)
            ig_out[at_rows, at] = total.astype(jnp.bfloat16)
            return 0

        lax.fori_loop(0, d_all // d_tile, out_tile, 0)
        return 0

    def sum_terms(term):
        total = term(0)
        for g in range(1, n_rep):
            total += term(g)
        return total

    def tail_term(g, j, at):
        return jnp.dot(masked[g, tail_rows, piece_at(j)], up_all[g, piece_at(j), at],
                       preferred_element_type=jnp.float32)

    def tail_tiles(visit):
        for i in range(d_all // d_tile):
            visit(pl.ds(i * d_tile, d_tile))

    def tail_first(g, ref, rows_at):
        def visit(at):
            ref[rows_at, at] = tail_term(g, 0, at)

        tail_tiles(visit)

    def tail_add(g, j, ref, rows_at):
        def visit(at):
            ref[rows_at, at] += tail_term(g, j, at)

        tail_tiles(visit)

    def tail_last(g, j):
        def visit(at):
            other = tail_term(g, j, at)
            if n_pieces > 1:
                other = other_sum[:, at] + other
            ig_out[tail_rows, at] = (own_sum[tail_rows, at] + other).astype(jnp.bfloat16)

        tail_tiles(visit)

    def own_tail():
        tail_first(rep, own_sum, tail_rows)

        def step(j, _):
            tail_add(rep, j, own_sum, tail_rows)
            return 0

        lax.fori_loop(1, n_pieces, step, 0)

    def other_tail(first, last):
        everything = pl.ds(0, CHUNK)

        def step(j, _):
            tail_arrived(j, 1)

            @pl.when(j == 0)
            def _():
                tail_first(1 - rep, other_sum, everything)

            @pl.when(j > 0)
            def _():
                tail_add(1 - rep, j, other_sum, everything)

            return 0

        lax.fori_loop(first, last, step, 0)

    def last_tail():
        tail_arrived(n_pieces - 1, 1)
        tail_last(1 - rep, n_pieces - 1)

    def finish_tail():
        for o in offsets:
            for j in range(n_pieces):
                tail_arrived(j, o)

        def visit(at):
            total = sum_terms(lambda g: jnp.dot(masked[g, tail_rows, :], up_all[g, :, at],
                                                preferred_element_type=jnp.float32))
            ig_out[tail_rows, at] = total.astype(jnp.bfloat16)

        tail_tiles(visit)

    first_late, last_late = z_own, n_z - (n_rep - 1)
    third = max(n_chunks // 3, 1)
    lax.fori_loop(0, z_own, make_terms, 0)
    lax.fori_loop(0, z_own, add_core, 0)
    loads[2].start()
    spread_start()
    loads[3].start()
    know_line()
    lax.fori_loop(1, 2, spread_z, 0)
    for part in range(z_own - 1):
        for o in offsets:
            early_copy(part, o, behind(o)).wait_recv()
    lax.fori_loop(first_late, last_late, make_terms, 0)
    lax.fori_loop(2, min(3, n_z), spread_z, 0)
    lax.fori_loop(first_late, last_late, add_core, 0)
    lax.fori_loop(1, 2, cross_x, 0)
    loads[2].wait()
    lax.fori_loop(0, third, chunk, 0)
    lax.fori_loop(third, 2 * third, chunk, 0)
    lax.fori_loop(0, z_own, add_x, 0)
    pass_core(my_z)
    lax.fori_loop(2 * third, tail, chunk, 0)
    tail_chunk()
    lax.fori_loop(last_late, n_z, make_terms, 0)
    lax.fori_loop(last_late, n_z, add_core, 0)
    lax.fori_loop(2, min(3, n_z), cross_x, 0)
    lax.fori_loop(first_late, last_late, add_x, 0)
    lax.fori_loop(3, n_z, spread_z, 0)
    lax.fori_loop(3, n_z, cross_x, 0)
    loads[3].wait()
    if n_rep == 2:
        lax.fori_loop(0, tail, own_part, 0)
        own_tail()
    lax.fori_loop(last_late, n_z, add_x, 0)
    lax.fori_loop(1, n_z, spread_core, 0)
    for o in offsets:
        all_of(up_all.at[behind(o), pl.ds(0, ff // 2)], uc_recv.at[o - 1])
    lax.fori_loop(0, tail, finish, 0)

    for o in offsets:
        for part in range(z_own - 1):
            early_copy(part, o, rep).wait_send()
        all_of(gfull.at[rep, :, last_cols], g_send.at[o - 1])
        up_rep_copy(o).wait_send()
        all_of(up_all.at[behind(o), pl.ds(0, ff // 2)], uc_send.at[o - 1])
        all_of(up_all.at[behind(o), pl.ds(0, ff // 4)], ux_send.at[o - 1])
    lax.fori_loop(0, n_z, spread_sent, 0)
    all_of(from_core, c_send)
    all_of(from_x, x_send)

    if n_rep == 2:
        other_tail(0, n_pieces - 2)

    total = from_x[my_z].astype(jnp.float32)
    all_of(from_z, z_recv)
    for o in range(n_z - 1):
        total += from_z[o].astype(jnp.float32)
    dg_out[...] = total / n_dp
    all_of(from_z, z_send)

    if n_rep == 2:
        other_tail(max(n_pieces - 2, 0), n_pieces - 1)
        last_tail()
    else:
        finish_tail()
    for o in offsets:
        all_of(masked.at[rep], p_send.at[o - 1])


def store(n_parts, ig, dg, ig_out, dg_out, sem):
    part = ig.shape[0] // n_parts
    copies = [pltpu.make_async_copy(ig.at[pl.ds(i * part, part)], ig_out.at[pl.ds(i * part, part)], sem.at[i])
              for i in range(n_parts)]
    copies.append(pltpu.make_async_copy(dg, dg_out, sem.at[n_parts]))
    for copy in copies:
        copy.start()
    for copy in copies:
        copy.wait()


def on_device(n_dp, n_rep, grad_out, pre_act, up_weight, down_weight, slot_counts):
    rows, d_own = grad_out.shape
    ff = pre_act.shape[1]
    d_all = down_weight.shape[0]
    n_z = n_dp // 4
    blk = d_all // n_dp
    n_chunks = rows // CHUNK
    n_pieces = ff // piece_of(ff)
    z_own, others = n_z // n_rep, n_rep - 1
    any_ref = pl.BlockSpec(memory_space=pl.ANY)
    in_vmem = pl.BlockSpec(memory_space=pltpu.VMEM)
    bf16, dma = jnp.bfloat16, pltpu.SemaphoreType.DMA
    results = pl.pallas_call(
        functools.partial(kernel, n_dp, n_rep),
        out_shape=(pltpu.VMEM((rows, d_all), bf16), pltpu.VMEM((blk, ff), jnp.float32)),
        in_specs=[pl.BlockSpec(memory_space=pltpu.SMEM)] + [any_ref] * 4,
        out_specs=(in_vmem,) * 2,
        scratch_shapes=[
            pltpu.VMEM((n_rep, rows, d_own), bf16),
            pltpu.VMEM((rows, ff), bf16),
            pltpu.VMEM((n_rep, ff, d_all), bf16),
            pltpu.VMEM((d_all, ff), bf16),
            pltpu.VMEM((n_z, 2, 2, blk, ff), bf16),
            pltpu.VMEM((n_z, 2, blk, ff), bf16),
            pltpu.VMEM((n_z, blk, ff), bf16),
            pltpu.VMEM((n_z - 1, blk, ff), bf16),
            pltpu.VMEM((n_rep, rows, ff), bf16),
            pltpu.VMEM((rows, d_all), jnp.float32),
            pltpu.VMEM((CHUNK, d_all), jnp.float32),
            pltpu.SemaphoreType.REGULAR((2,)),
            dma((4,)), dma((max(z_own - 1, 1), others)), dma((max(z_own - 1, 1), others)),
            dma((others,)), dma((n_chunks, others)),
            dma((others,)), dma((n_chunks - 1, others)), dma((n_pieces, others)),
            dma((others,)), dma((n_z + 1, others)), dma((others,)), dma((others,)),
            dma((2 * n_z, others)), dma((others,)),
            dma, dma((n_z,)), dma, dma((n_z,)), dma, dma,
        ],
        compiler_params=pltpu.CompilerParams(
            collective_id=0, has_side_effects=True, vmem_limit_bytes=56 * 2**20),
    )(slot_counts, grad_out, pre_act, up_weight, down_weight)
    n_parts = 4
    return pl.pallas_call(
        functools.partial(store, n_parts),
        out_shape=(jax.ShapeDtypeStruct((rows, d_all), bf16), jax.ShapeDtypeStruct((blk, ff), jnp.float32)),
        in_specs=[in_vmem] * 2,
        out_specs=(any_ref,) * 2,
        scratch_shapes=[dma((n_parts + 1,))],
        compiler_params=pltpu.CompilerParams(vmem_limit_bytes=6 * 2**20),
    )(*results)


def solution(mesh):
    sizes = dict(mesh.shape)
    return jax.shard_map(
        functools.partial(on_device, sizes["dp"], sizes["rep"]),
        mesh=mesh,
        in_specs=(P("dp", "rep"), P("dp", "rep"), P("rep", None), P(None, "rep"), P("dp")),
        out_specs=(P("dp", None), P("dp", "rep")),
        check_vma=False,
    )
```

```python
import functools

import jax
import jax.numpy as jnp
from jax import lax
from jax.experimental import pallas as pl
from jax.experimental.pallas import tpu as pltpu
from jax.sharding import PartitionSpec as P

MESH = pl.DeviceIdType.MESH
CHUNK = 128


def tile_of(extent):
    return next(t for t in (512, 384, 256, 128) if extent % t == 0)


def piece_of(extent):
    return next(t for t in (256, 128) if extent % t == 0)


def kernel(n_dp, n_rep, counts, grad, pre, up, down, ig_out, dg_out,
           gfull, hid, up_all, down_v, terms, from_core, from_x, from_z, masked, own_sum, other_sum,
           in_sem, load_sem, gp_send, gp_recv, g_send, g_recv, p_send, p_recv, t_recv, uy_send, uz_send, ux_send,
           uc_send, u_recv, uc_recv, c_send, c_recv, x_send, x_recv, z_send, z_recv):
    rows, d_own = grad.shape
    ff = pre.shape[1]
    d_all = down.shape[0]
    n_z = n_dp // 4
    z_own = n_z // n_rep
    blk = d_all // n_dp
    n_chunks = rows // CHUNK
    ff_tile, d_tile = tile_of(ff), tile_of(d_all)
    n_tiles = ff // ff_tile
    piece = piece_of(ff)
    n_pieces = ff // piece
    slice_rows = n_dp
    while ff % (slice_rows * 16):
        slice_rows //= 2
    slice_cols = n_dp // slice_rows
    tall, wide = ff // slice_rows, d_all // slice_cols

    me = lax.axis_index("dp")
    rep = lax.axis_index("rep")
    my_z, my_x, my_c = me // 4, (me // 2) % 2, me % 2
    core_peer = {"dp": my_z * 4 + my_x * 2 + (1 - my_c)}
    x_peer = {"dp": my_z * 4 + (1 - my_x) * 2 + my_c}
    offsets = range(1, n_rep)
    above, below = my_z + 1 < n_z, my_z > 0

    def ahead(o):
        return lax.rem(rep + o, n_rep)

    def behind(o):
        return lax.rem(rep + n_rep - o, n_rep)

    def send(src, dst, send_sem, recv_sem, peer):
        return pltpu.make_async_remote_copy(src_ref=src, dst_ref=dst, send_sem=send_sem, recv_sem=recv_sem,
                                            device_id=peer, device_id_type=MESH)

    def all_of(ref, sem):
        pltpu.make_async_copy(ref, ref, sem).wait()

    def z_peer(z):
        return {"dp": z * 4 + my_x * 2 + my_c}

    def signal(sem, peer):
        pl.semaphore_signal(sem, inc=1, device_id=peer, device_id_type=MESH)

    barrier = pltpu.get_barrier_semaphore()
    for o in offsets:
        signal(barrier, {"rep": ahead(o)})
    pl.when(my_x == 0)(lambda: signal(barrier, x_peer))
    pl.when(my_c == 0)(lambda: signal(barrier, core_peer))
    pl.when(above)(lambda: signal(barrier, z_peer(my_z + 1)))

    loads = [
        pltpu.make_async_copy(src, dst, load_sem.at[i])
        for i, (src, dst) in enumerate(
            ((grad, gfull.at[rep]), (pre, hid), (down, down_v), (up, up_all.at[rep])))
    ]
    loads[0].start()
    loads[1].start()
    pl.semaphore_wait(barrier, n_rep - 1 + my_x + my_c + below.astype(jnp.int32))

    def rows_of(c):
        return pl.ds(pl.multiple_of(c * CHUNK, CHUNK), CHUNK)

    last_cols = pl.ds((z_own - 1) * 4 * blk, 4 * blk)

    def grad_copy(c, o, source):
        return send(gfull.at[rep, rows_of(c), last_cols], gfull.at[source, rows_of(c), last_cols],
                    g_send.at[o - 1], g_recv.at[c, o - 1], {"rep": ahead(o)})

    def early_copy(part, o, source):
        cols = pl.ds(part * 4 * blk, 4 * blk)
        return send(gfull.at[rep, :, cols], gfull.at[source, :, cols],
                    gp_send.at[part, o - 1], gp_recv.at[part, o - 1], {"rep": ahead(o)})

    def tile_at(j):
        return pl.ds(pl.multiple_of(j * ff_tile, ff_tile), ff_tile)

    def piece_at(j):
        return pl.ds(pl.multiple_of(j * piece, piece), piece)

    def part_copy(c, j, o):
        block = masked.at[rep, rows_of(c), tile_at(j)]
        return send(block, block, p_send.at[o - 1], p_recv.at[c, o - 1], {"rep": ahead(o)})

    def tail_copy(j, o):
        block = masked.at[rep, tail_rows, piece_at(j)]
        return send(block, block, p_send.at[o - 1], t_recv.at[j, o - 1], {"rep": ahead(o)})

    def tail_arrived(j, o):
        all_of(masked.at[behind(o), tail_rows, piece_at(j)], t_recv.at[j, o - 1])

    def slice_at(s):
        down_at = pl.ds(pl.multiple_of((s // slice_cols) * tall, tall), tall)
        if slice_cols == 1:
            return (down_at,)
        return (down_at, pl.ds(pl.multiple_of((s % slice_cols) * wide, wide), wide))

    def index_of(z, x, core):
        return z * 4 + x * 2 + core

    def up_rep_copy(o):
        return send(up.at[slice_at(me)], up_all.at[(rep,) + slice_at(me)],
                    uy_send.at[o - 1], u_recv.at[my_z * 2 + my_x, o - 1], {"rep": ahead(o)})

    def up_copy(o, s, send_sem, peer):
        block = up_all.at[(behind(o),) + slice_at(s)]
        return send(block, block, send_sem, u_recv.at[s // 2, o - 1], peer)

    def along_z(o, z, step):
        to = lax.rem(my_z + step + n_z, n_z)
        stage = z if step > 0 else jnp.where(z == my_z, n_z, z)
        return up_copy(o, index_of(z, my_x, my_c), uz_send.at[stage, o - 1], z_peer(to))

    def over_x(o, z):
        return up_copy(o, index_of(z, my_x, my_c), ux_send.at[o - 1], x_peer)

    def over_core(o, z, x):
        block = up_all.at[(behind(o),) + slice_at(index_of(z, x, my_c))]
        return send(block, block, uc_send.at[o - 1], uc_recv.at[o - 1], core_peer)

    def landed(o, z, x):
        up_copy(o, index_of(z, x, my_c), ux_send.at[o - 1], x_peer).wait_recv()

    for o in offsets:
        up_rep_copy(o).start()
    loads[0].wait()
    for part in range(z_own - 1):
        for o in offsets:
            early_copy(part, o, rep).start()
    for c in range(n_chunks):
        for o in offsets:
            grad_copy(c, o, rep).start()
    pl.when(my_c == 1)(lambda: signal(in_sem.at[0], core_peer))
    pl.when(my_x == 1)(lambda: signal(in_sem.at[1], x_peer))
    pl.when(my_z == n_z - 1)(lambda: signal(in_sem.at[2], z_peer(my_z - 1)))

    loads[1].wait()
    count = counts[0]

    def mask_rows(c, _):
        at = lax.broadcasted_iota(jnp.int32, (CHUNK, ff), 0) + c * CHUNK
        kept = jnp.where(at < count, hid[rows_of(c), :].astype(jnp.float32), 0.0)
        kept = jnp.maximum(kept, 0.0)
        hid[rows_of(c), :] = kept.astype(jnp.bfloat16)
        return 0

    lax.fori_loop(0, n_chunks, mask_rows, 0)

    def know_core():
        pl.when(my_c == 0)(lambda: pl.semaphore_wait(in_sem.at[0], 1))

    def know_x():
        pl.when(my_x == 0)(lambda: pl.semaphore_wait(in_sem.at[1], 1))

    def know_above():
        @pl.when(above)
        def _():
            pl.semaphore_wait(in_sem.at[2], 1)
            pl.when(below)(lambda: signal(in_sem.at[2], z_peer(my_z - 1)))

    def know_below():
        pl.when(below)(lambda: pl.semaphore_wait(in_sem.at[3], 1))
        pl.when(above)(lambda: signal(in_sem.at[3], z_peer(my_z + 1)))

    def core_copy(z):
        return send(terms.at[z, 1 - my_c], from_core.at[z], c_send, c_recv.at[z], core_peer)

    def x_copy(z):
        return send(from_core.at[z, 1 - my_x], from_x.at[z], x_send, x_recv.at[z], x_peer)

    def z_copy(z, source):
        slot = jnp.where(source > z, source - 1, source)
        return send(from_x.at[z], from_z.at[slot], z_send, z_recv, z_peer(z))

    def z_at(k):
        late = k - z_own
        other = lax.rem(rep + 1 + lax.rem(late, n_rep - 1), n_rep) * z_own + late // (n_rep - 1)
        return jnp.where(k < z_own, rep * z_own + k, other)

    def make_terms(k, _):
        z = z_at(k)
        group = z // z_own
        cols = pl.ds(pl.multiple_of((z - group * z_own) * 4 * blk, 4 * blk), 4 * blk)

        def one(j, _):
            at = tile_at(j)
            out = lax.dot_general(
                gfull[group, :, cols], hid[:, at], (((0,), (0,)), ((), ())),
                preferred_element_type=jnp.float32).astype(jnp.bfloat16)
            for x in range(2):
                for core in range(2):
                    row = (x * 2 + core) * blk
                    terms[z, core, x, :, at] = out[row:row + blk]
            return 0

        lax.fori_loop(0, n_tiles, one, 0)
        core_copy(z).start()
        return 0

    def add_core(k, _):
        z = z_at(k)
        core_copy(z).wait_recv()
        for x in range(2):
            total = from_core[z, x].astype(jnp.float32) + terms[z, my_c, x].astype(jnp.float32)
            from_core[z, x] = total.astype(jnp.bfloat16)
        x_copy(z).start()
        return 0

    def add_x(k, _):
        z = z_at(k)
        x_copy(z).wait_recv()
        total = from_x[z].astype(jnp.float32) + from_core[z, my_x].astype(jnp.float32)
        from_x[z] = total.astype(jnp.bfloat16)

        @pl.when(z != my_z)
        def _():
            z_copy(z, my_z).start()

        return 0

    tail = n_chunks - 1
    tail_rows = rows_of(tail)

    def hidden_part(at_rows, at):
        total = jnp.dot(gfull[0, at_rows, :], down_v[:d_own, at], preferred_element_type=jnp.float32)
        for g in range(1, n_rep):
            total += jnp.dot(gfull[g, at_rows, :], down_v[g * d_own:(g + 1) * d_own, at],
                             preferred_element_type=jnp.float32)
        passed = hid[at_rows, at].astype(jnp.float32) > 0.0
        masked[rep, at_rows, at] = jnp.where(passed, total, 0.0).astype(jnp.bfloat16)

    def grads_arrived(c):
        for o in offsets:
            grad_copy(c, o, behind(o)).wait_recv()

    def chunk(c, _):
        grads_arrived(c)

        def hidden_tile(j, _):
            hidden_part(rows_of(c), tile_at(j))
            for o in offsets:
                part_copy(c, j, o).start()
            return 0

        lax.fori_loop(0, n_tiles, hidden_tile, 0)
        return 0

    def tail_chunk():
        grads_arrived(tail)

        def hidden_piece(j, _):
            hidden_part(tail_rows, piece_at(j))
            for o in offsets:
                tail_copy(j, o).start()
            return 0

        lax.fori_loop(0, n_pieces, hidden_piece, 0)

    def own_part(c, _):
        def own_tile(j, _):
            at = pl.ds(pl.multiple_of(j * d_tile, d_tile), d_tile)
            own_sum[rows_of(c), at] = jnp.dot(masked[rep, rows_of(c), :], up_all[rep, :, at],
                                              preferred_element_type=jnp.float32)
            return 0

        lax.fori_loop(0, d_all // d_tile, own_tile, 0)
        return 0

    def spread_start():
        for o in offsets:
            landed(o, my_z, my_x)
            pl.when(above)(lambda: along_z(o, my_z, 1).start())
            pl.when(below)(lambda: along_z(o, my_z, -1).start())
            over_x(o, my_z).start()
            over_core(o, my_z, my_x).start()

    def both_sides(d, visit):
        pl.when(my_z >= d)(lambda: visit(my_z - d, above, 1))
        pl.when(my_z + d < n_z)(lambda: visit(my_z + d, below, -1))

    def spread_z(d, _):
        def visit(z, goes_on, step):
            for o in offsets:
                landed(o, z, my_x)
                pl.when(goes_on)(lambda: along_z(o, z, step).start())
                over_core(o, z, my_x).start()

        both_sides(d, visit)
        return 0

    def cross_x(d, _):
        def visit(z, goes_on, step):
            for o in offsets:
                over_x(o, z).start()

        both_sides(d, visit)
        return 0

    def pass_core(z):
        for o in offsets:
            landed(o, z, 1 - my_x)
            over_core(o, z, 1 - my_x).start()

    def spread_core(d, _):
        both_sides(d, lambda z, goes_on, step: pass_core(z))
        return 0

    def spread_sent(z, _):
        for o in offsets:
            pl.when((z <= my_z) & above)(lambda: along_z(o, z, 1).wait_send())
            pl.when((z >= my_z) & below)(lambda: along_z(o, z, -1).wait_send())
        return 0

    def finish(c, _):
        at_rows = rows_of(c)
        for o in offsets:
            all_of(masked.at[behind(o), at_rows], p_recv.at[c, o - 1])

        def out_tile(j, _):
            at = pl.ds(pl.multiple_of(j * d_tile, d_tile), d_tile)

            def term(g):
                return jnp.dot(masked[g, at_rows, :], up_all[g, :, at], preferred_element_type=jnp.float32)

            if n_rep == 2:
                total = own_sum[at_rows, at] + term(1 - rep)
            else:
                total = sum_terms(term)
            ig_out[at_rows, at] = total.astype(jnp.bfloat16)
            return 0

        lax.fori_loop(0, d_all // d_tile, out_tile, 0)
        return 0

    def sum_terms(term):
        total = term(0)
        for g in range(1, n_rep):
            total += term(g)
        return total

    def tail_term(g, j, at):
        return jnp.dot(masked[g, tail_rows, piece_at(j)], up_all[g, piece_at(j), at],
                       preferred_element_type=jnp.float32)

    def tail_tiles(visit):
        for i in range(d_all // d_tile):
            visit(pl.ds(i * d_tile, d_tile))

    def tail_first(g, ref, rows_at):
        def visit(at):
            ref[rows_at, at] = tail_term(g, 0, at)

        tail_tiles(visit)

    def tail_add(g, j, ref, rows_at):
        def visit(at):
            ref[rows_at, at] += tail_term(g, j, at)

        tail_tiles(visit)

    def tail_last(g, j):
        def visit(at):
            other = tail_term(g, j, at)
            if n_pieces > 1:
                other = other_sum[:, at] + other
            ig_out[tail_rows, at] = (own_sum[tail_rows, at] + other).astype(jnp.bfloat16)

        tail_tiles(visit)

    def own_tail():
        tail_first(rep, own_sum, tail_rows)

        def step(j, _):
            tail_add(rep, j, own_sum, tail_rows)
            return 0

        lax.fori_loop(1, n_pieces, step, 0)

    def other_tail(first, last):
        everything = pl.ds(0, CHUNK)

        def step(j, _):
            tail_arrived(j, 1)

            @pl.when(j == 0)
            def _():
                tail_first(1 - rep, other_sum, everything)

            @pl.when(j > 0)
            def _():
                tail_add(1 - rep, j, other_sum, everything)

            return 0

        lax.fori_loop(first, last, step, 0)

    def last_tail():
        tail_arrived(n_pieces - 1, 1)
        tail_last(1 - rep, n_pieces - 1)

    def finish_tail():
        for o in offsets:
            for j in range(n_pieces):
                tail_arrived(j, o)

        def visit(at):
            total = sum_terms(lambda g: jnp.dot(masked[g, tail_rows, :], up_all[g, :, at],
                                                preferred_element_type=jnp.float32))
            ig_out[tail_rows, at] = total.astype(jnp.bfloat16)

        tail_tiles(visit)

    first_late, last_late = z_own, n_z - (n_rep - 1)
    third = max(n_chunks // 3, 1)
    know_core()
    lax.fori_loop(0, z_own, make_terms, 0)
    know_x()
    know_above()
    lax.fori_loop(0, z_own, add_core, 0)
    loads[2].start()
    spread_start()
    loads[3].start()
    know_below()
    lax.fori_loop(1, 2, spread_z, 0)
    for part in range(z_own - 1):
        for o in offsets:
            early_copy(part, o, behind(o)).wait_recv()
    lax.fori_loop(first_late, last_late, make_terms, 0)
    lax.fori_loop(2, min(3, n_z), spread_z, 0)
    lax.fori_loop(first_late, last_late, add_core, 0)
    lax.fori_loop(1, 2, cross_x, 0)
    loads[2].wait()
    lax.fori_loop(0, third, chunk, 0)
    lax.fori_loop(third, 2 * third, chunk, 0)
    lax.fori_loop(0, z_own, add_x, 0)
    pass_core(my_z)
    lax.fori_loop(2 * third, tail, chunk, 0)
    tail_chunk()
    lax.fori_loop(last_late, n_z, make_terms, 0)
    lax.fori_loop(last_late, n_z, add_core, 0)
    lax.fori_loop(2, min(3, n_z), cross_x, 0)
    lax.fori_loop(first_late, last_late, add_x, 0)
    lax.fori_loop(3, n_z, spread_z, 0)
    lax.fori_loop(3, n_z, cross_x, 0)
    loads[3].wait()
    if n_rep == 2:
        lax.fori_loop(0, tail, own_part, 0)
        own_tail()
    lax.fori_loop(last_late, n_z, add_x, 0)
    lax.fori_loop(1, n_z, spread_core, 0)
    for o in offsets:
        all_of(up_all.at[behind(o), pl.ds(0, ff // 2)], uc_recv.at[o - 1])
    lax.fori_loop(0, tail, finish, 0)

    for o in offsets:
        for part in range(z_own - 1):
            early_copy(part, o, rep).wait_send()
        all_of(gfull.at[rep, :, last_cols], g_send.at[o - 1])
        up_rep_copy(o).wait_send()
        all_of(up_all.at[behind(o), pl.ds(0, ff // 2)], uc_send.at[o - 1])
        all_of(up_all.at[behind(o), pl.ds(0, ff // 4)], ux_send.at[o - 1])
    lax.fori_loop(0, n_z, spread_sent, 0)
    all_of(from_core, c_send)
    all_of(from_x, x_send)

    if n_rep == 2:
        other_tail(0, n_pieces - 2)

    total = from_x[my_z].astype(jnp.float32)
    all_of(from_z, z_recv)
    for o in range(n_z - 1):
        total += from_z[o].astype(jnp.float32)
    dg_out[...] = total / n_dp
    all_of(from_z, z_send)

    if n_rep == 2:
        other_tail(max(n_pieces - 2, 0), n_pieces - 1)
        last_tail()
    else:
        finish_tail()
    for o in offsets:
        all_of(masked.at[rep], p_send.at[o - 1])


def store(n_parts, ig, dg, ig_out, dg_out, sem):
    part = ig.shape[0] // n_parts
    copies = [pltpu.make_async_copy(ig.at[pl.ds(i * part, part)], ig_out.at[pl.ds(i * part, part)], sem.at[i])
              for i in range(n_parts)]
    copies.append(pltpu.make_async_copy(dg, dg_out, sem.at[n_parts]))
    for copy in copies:
        copy.start()
    for copy in copies:
        copy.wait()


def on_device(n_dp, n_rep, grad_out, pre_act, up_weight, down_weight, slot_counts):
    rows, d_own = grad_out.shape
    ff = pre_act.shape[1]
    d_all = down_weight.shape[0]
    n_z = n_dp // 4
    blk = d_all // n_dp
    n_chunks = rows // CHUNK
    n_pieces = ff // piece_of(ff)
    z_own, others = n_z // n_rep, n_rep - 1
    any_ref = pl.BlockSpec(memory_space=pl.ANY)
    in_vmem = pl.BlockSpec(memory_space=pltpu.VMEM)
    bf16, dma = jnp.bfloat16, pltpu.SemaphoreType.DMA
    results = pl.pallas_call(
        functools.partial(kernel, n_dp, n_rep),
        out_shape=(pltpu.VMEM((rows, d_all), bf16), pltpu.VMEM((blk, ff), jnp.float32)),
        in_specs=[pl.BlockSpec(memory_space=pltpu.SMEM)] + [any_ref] * 4,
        out_specs=(in_vmem,) * 2,
        scratch_shapes=[
            pltpu.VMEM((n_rep, rows, d_own), bf16),
            pltpu.VMEM((rows, ff), bf16),
            pltpu.VMEM((n_rep, ff, d_all), bf16),
            pltpu.VMEM((d_all, ff), bf16),
            pltpu.VMEM((n_z, 2, 2, blk, ff), bf16),
            pltpu.VMEM((n_z, 2, blk, ff), bf16),
            pltpu.VMEM((n_z, blk, ff), bf16),
            pltpu.VMEM((n_z - 1, blk, ff), bf16),
            pltpu.VMEM((n_rep, rows, ff), bf16),
            pltpu.VMEM((rows, d_all), jnp.float32),
            pltpu.VMEM((CHUNK, d_all), jnp.float32),
            pltpu.SemaphoreType.REGULAR((4,)),
            dma((4,)), dma((max(z_own - 1, 1), others)), dma((max(z_own - 1, 1), others)),
            dma((others,)), dma((n_chunks, others)),
            dma((others,)), dma((n_chunks - 1, others)), dma((n_pieces, others)),
            dma((others,)), dma((n_z + 1, others)), dma((others,)), dma((others,)),
            dma((2 * n_z, others)), dma((others,)),
            dma, dma((n_z,)), dma, dma((n_z,)), dma, dma,
        ],
        compiler_params=pltpu.CompilerParams(
            collective_id=0, has_side_effects=True, vmem_limit_bytes=56 * 2**20),
    )(slot_counts, grad_out, pre_act, up_weight, down_weight)
    n_parts = 4
    return pl.pallas_call(
        functools.partial(store, n_parts),
        out_shape=(jax.ShapeDtypeStruct((rows, d_all), bf16), jax.ShapeDtypeStruct((blk, ff), jnp.float32)),
        in_specs=[in_vmem] * 2,
        out_specs=(any_ref,) * 2,
        scratch_shapes=[dma((n_parts + 1,))],
        compiler_params=pltpu.CompilerParams(vmem_limit_bytes=6 * 2**20),
    )(*results)


def solution(mesh):
    sizes = dict(mesh.shape)
    return jax.shard_map(
        functools.partial(on_device, sizes["dp"], sizes["rep"]),
        mesh=mesh,
        in_specs=(P("dp", "rep"), P("dp", "rep"), P("rep", None), P(None, "rep"), P("dp")),
        out_specs=(P("dp", None), P("dp", "rep")),
        check_vma=False,
    )
```
